32 devices in a mesh: dp: 16 (over z, y, core), pipe: 2 (over x).
Axes of the slice: x: 2, y: 2, z: 4, core: 2. Of those that a mesh axis runs over, the one named last changes fastest.
Arguments:
- clean: bfloat16 [64, 128, 320], P('dp'), may hold values from -20 to 20
- noise: bfloat16 [64, 128, 320], P('dp'), may hold values from -6 to 6
- timesteps: int32 [64], P('dp'), may hold values from 0 to 999
- enc_in: bfloat16 [2, 320, 1280], P('pipe'), may hold values from -0.3125 to 0.3125
- enc_out: bfloat16 [2, 1280, 320], P('pipe'), may hold values from -0.15625 to 0.15625
- enc_gain: float32 [2, 320], P('pipe'), may hold values from 0.5 to 1.5
- time_gain: float32 [2, 320], P('pipe'), may hold values from -3 to 3
- dec_w: bfloat16 [2, 640, 320], P('pipe'), may hold values from -0.25 to 0.25
- dec_gain: float32 [2, 640], P('pipe'), may hold values from 0.5 to 1.5
Outputs:
- loss: float32 [], replicated
- grad_enc_in: bfloat16 [2, 320, 1280], P('pipe')
- grad_enc_out: bfloat16 [2, 1280, 320], P('pipe')
- grad_enc_gain: float32 [2, 320], P('pipe')
- grad_dec_w: bfloat16 [2, 640, 320], P('pipe')
- grad_dec_gain: float32 [2, 640], P('pipe')
The draws below stay inside these ranges and needn't reach their ends.
All inputs are finite; a program needn't handle non-finite values.
Results may differ from the reference program's by a relative error of at most 0.004.
Values may be sent and summed in bfloat16 or wider, within the bound.
No kernel may reach another device: no remote copies, remote signals or barrier semaphores. Data moves between devices by JAX's collectives and lax.ppermute only.
A program may use at most 64 MiB of HBM per device.

```python
import math
import jax
import jax.numpy as jnp
from jax import lax

C = 320
H = 1280
ROWS = 128
TSTEPS = 1000
LEVELS = 2
SAMPLES = 64


def draw_clean(key, part):
    key_base, key_row, key_col = jax.random.split(key, 3)
    row_scale = jnp.exp(jax.random.uniform(key_row, (SAMPLES, ROWS, 1), minval=0.0, maxval=jnp.log(10.0)))
    col_scale = jnp.exp(jax.random.uniform(key_col, (1, 1, C), minval=jnp.log(0.5), maxval=jnp.log(2.0)))
    values = jax.random.truncated_normal(key_base, -4.0, 4.0, (SAMPLES, ROWS, C))
    return (0.25 * values * row_scale * col_scale).astype(jnp.float32).astype(jnp.bfloat16)


def with_ends(result, stream_key, least, high):
    index_at = [jax.random.randint(jax.random.fold_in(stream_key, axis), (), 0, length) for axis, length in enumerate(result.shape)]
    widest = result.shape.index(max(result.shape))
    beside = index_at[:widest] + [(index_at[widest] + 1) % result.shape[widest]] + index_at[widest + 1:]
    return result.at[tuple(index_at)].set(least).at[tuple(beside)].set(high)


def shard_levels(rng, shape, pieces, least, largest):
    level = 1.0
    for position, shards_of in pieces:
        draws = jax.random.uniform(jax.random.fold_in(jax.random.fold_in(rng, 6), position), (shards_of,), jnp.float32, least / len(pieces), largest / len(pieces))
        level = level * jnp.repeat(jnp.exp(draws), shape[position] // shards_of).reshape((-1,) + (1,) * (len(shape) - 1 - position))
    return level


def normal_values(rng, extent, scale, reach, pieces=(), kind=jnp.bfloat16):
    drawn = jax.random.normal(rng, extent, jnp.float32) * scale
    if len(pieces) > 0:
        drawn = shard_levels(rng, extent, pieces, -0.22, 0.18) * drawn
    return jnp.clip(drawn, min=-reach, max=reach).astype(kind)


def setup_inputs(seed: int = 0) -> dict:
    streams_of = jax.random.split(jax.random.key(seed), 10)
    clean = draw_clean(jax.random.fold_in(streams_of[9], 71), 0)
    noise = normal_values(streams_of[1], (SAMPLES, ROWS, C), 1.0, 6.0, ((0, 16),))
    timesteps = with_ends(jax.random.randint(streams_of[2], (SAMPLES,), 0, TSTEPS), jax.random.fold_in(streams_of[2], 1), 0, TSTEPS - 1).astype(jnp.int32)
    enc_in = normal_values(streams_of[3], (LEVELS, C, H), C ** -0.5, 0.3125, ((0, 2),))
    enc_out = normal_values(streams_of[4], (LEVELS, H, C), H ** -0.5, 0.15625, ((0, 2),))
    enc_gain = jnp.clip(1.0 + 0.1 * jax.random.normal(streams_of[5], (LEVELS, C), jnp.float32), 0.5, 1.5)
    time_gain = normal_values(streams_of[6], (LEVELS, C), 0.5, 3.0, ((0, 2),), jnp.float32)
    dec_w = normal_values(streams_of[7], (LEVELS, 2 * C, C), (2 * C) ** -0.5, 0.25, ((0, 2),))
    dec_gain = jnp.clip(1.0 + 0.1 * jax.random.normal(streams_of[8], (LEVELS, 2 * C), jnp.float32), 0.5, 1.5)
    return {"clean": clean, "noise": noise, "timesteps": timesteps, "enc_in": enc_in, "enc_out": enc_out, "enc_gain": enc_gain, "time_gain": time_gain, "dec_w": dec_w, "dec_gain": dec_gain}


EPS = 1e-06
GELU_SCALE = math.sqrt(2.0 / math.pi)
CUBIC = 0.044715

def left_dot(matrix_a, matrix_b):
    return lax.dot_general(matrix_a, matrix_b, (((0,), (0,)), ((), ())), preferred_element_type=jnp.float32)

def right_dot(matrix_a, matrix_b):
    return lax.dot_general(matrix_a, matrix_b, (((1,), (1,)), ((), ())), preferred_element_type=jnp.float32)

def plan(step_ids):
    angles = 0.5 * math.pi * (step_ids.astype(jnp.float32) + 0.5) / TSTEPS
    return (jnp.cos(angles), jnp.sin(angles))

def features(step_ids, channels):
    half_width = channels // 2
    frequency = jnp.exp(-math.log(10000.0) * jnp.arange(half_width, dtype=jnp.float32) / half_width)
    angles = step_ids.astype(jnp.float32)[:, None] * frequency[None, :]
    return jnp.concatenate([jnp.sin(angles), jnp.cos(angles)], axis=1)

def normalize(inputs):
    values = inputs.astype(jnp.float32)
    inverse = lax.rsqrt(lax.optimization_barrier(jnp.mean(values * values, axis=-1, keepdims=True)) + EPS)
    return (values * inverse, inverse)

def norm_back(grad_unit, unit_rows, inverse):
    return (grad_unit - unit_rows * lax.optimization_barrier(jnp.mean(grad_unit * unit_rows, axis=-1, keepdims=True))) * inverse

def gelu_value(pre_act):
    inner = GELU_SCALE * (pre_act + CUBIC * pre_act * pre_act * pre_act)
    return 0.5 * pre_act * (1.0 + jnp.tanh(inner))

def gelu_slope(pre_act):
    tanh_val = jnp.tanh(GELU_SCALE * (pre_act + CUBIC * pre_act * pre_act * pre_act))
    return 0.5 * (1.0 + tanh_val) + 0.5 * pre_act * (1.0 - tanh_val * tanh_val) * GELU_SCALE * (1.0 + 3.0 * CUBIC * pre_act * pre_act)

def encode_parts(inputs, embedding, norm_gain, weight_in):
    unit_rows, inverse = normalize(inputs)
    normed = (unit_rows * norm_gain + embedding).astype(jnp.bfloat16)
    pre_act = jnp.dot(normed, weight_in, preferred_element_type=jnp.float32)
    hidden = gelu_value(pre_act).astype(jnp.bfloat16)
    return (unit_rows, inverse, normed, pre_act, hidden)

def encode(inputs, embedding, norm_gain, weight_in, weight_out):
    hidden = encode_parts(inputs, embedding, norm_gain, weight_in)[4]
    return (inputs.astype(jnp.float32) + jnp.dot(hidden, weight_out, preferred_element_type=jnp.float32)).astype(jnp.bfloat16)

def encode_back(inputs, embedding, norm_gain, weight_in, weight_out, grad_y):
    unit_rows, inverse, normed, pre_act, hidden = encode_parts(inputs, embedding, norm_gain, weight_in)
    grad_out = left_dot(hidden, grad_y)
    grad_hidden = right_dot(grad_y, weight_out)
    grad_pre = (grad_hidden * gelu_slope(pre_act)).astype(jnp.bfloat16)
    grad_in = left_dot(normed, grad_pre)
    grad_normed = right_dot(grad_pre, weight_in)
    grad_gain = lax.optimization_barrier(jnp.sum(grad_normed * unit_rows, axis=0))
    grad_x = grad_y.astype(jnp.float32) + norm_back(grad_normed * norm_gain, unit_rows, inverse)
    return (grad_x, grad_in, grad_out, grad_gain)

def decode_parts(inputs, skip_rows, norm_gain):
    channels = inputs.shape[-1]
    unit_x, inv_x = normalize(inputs)
    unit_s, inv_s = normalize(skip_rows)
    joined = jnp.concatenate([unit_x * norm_gain[:channels], unit_s * norm_gain[channels:]], axis=-1).astype(jnp.bfloat16)
    return (unit_x, inv_x, unit_s, inv_s, joined)

def decode(inputs, skip_rows, norm_gain, weight):
    joined = decode_parts(inputs, skip_rows, norm_gain)[4]
    return (inputs.astype(jnp.float32) + jnp.dot(joined, weight, preferred_element_type=jnp.float32)).astype(jnp.bfloat16)

def decode_back(inputs, skip_rows, norm_gain, weight, grad_y):
    channels = inputs.shape[-1]
    unit_x, inv_x, unit_s, inv_s, joined = decode_parts(inputs, skip_rows, norm_gain)
    grad_weight = left_dot(joined, grad_y)
    grad_joined = right_dot(grad_y, weight)
    grad_gain = lax.optimization_barrier(jnp.sum(grad_joined * jnp.concatenate([unit_x, unit_s], axis=-1), axis=0))
    scaled = grad_joined * norm_gain
    grad_x = grad_y.astype(jnp.float32) + norm_back(scaled[:, :channels], unit_x, inv_x)
    grad_skip = norm_back(scaled[:, channels:], unit_s, inv_s)
    return (grad_x, grad_skip, grad_weight, grad_gain)

def reference(clean, noise, timesteps, enc_in, enc_out, enc_gain, time_gain, dec_w, dec_gain):
    keep_rate, spread = plan(timesteps)
    keep_full = keep_rate[:, None, None]
    spread_full = spread[:, None, None]
    clean_f = clean.astype(jnp.float32)
    noise_f = noise.astype(jnp.float32)
    acts = (keep_full * clean_f + spread_full * noise_f).astype(jnp.bfloat16).reshape(-1, C)
    target = (keep_full * noise_f - spread_full * clean_f).reshape(-1, C)
    feats = features(timesteps, C)
    embeds = [jnp.repeat(time_gain[section][None, :] * feats, ROWS, axis=0) for section in range(LEVELS)]
    enc_keep = []
    for section in range(LEVELS):
        enc_keep.append(acts)
        acts = encode(acts, embeds[section], enc_gain[section], enc_in[section], enc_out[section])
    dec_keep = [None] * LEVELS
    for section in reversed(range(LEVELS)):
        dec_keep[section] = acts
        acts = decode(acts, enc_keep[section], dec_gain[section], dec_w[section])
    residual = acts.astype(jnp.float32) - target
    loss_value = jnp.sum(residual * residual) / (SAMPLES * ROWS * C)
    grad_y = (residual / math.sqrt(SAMPLES * ROWS)).astype(jnp.bfloat16)
    skip_grads = [None] * LEVELS
    dec_weight_grads = [None] * LEVELS
    dec_gain_grads = [None] * LEVELS
    for section in range(LEVELS):
        grad_x, grad_skip, grad_weight, grad_gain = decode_back(dec_keep[section], enc_keep[section], dec_gain[section], dec_w[section], grad_y)
        skip_grads[section] = grad_skip
        dec_weight_grads[section] = grad_weight
        dec_gain_grads[section] = grad_gain
        grad_y = grad_x.astype(jnp.bfloat16)
    in_grads = [None] * LEVELS
    out_grads = [None] * LEVELS
    gain_grads = [None] * LEVELS
    for section in reversed(range(LEVELS)):
        grad_x, grad_in, grad_out, grad_gain = encode_back(enc_keep[section], embeds[section], enc_gain[section], enc_in[section], enc_out[section], grad_y)
        in_grads[section] = grad_in
        out_grads[section] = grad_out
        gain_grads[section] = grad_gain
        grad_y = (grad_x + skip_grads[section]).astype(jnp.bfloat16)
    return (loss_value, jnp.stack(in_grads).astype(jnp.bfloat16), jnp.stack(out_grads).astype(jnp.bfloat16), jnp.stack(gain_grads), jnp.stack(dec_weight_grads).astype(jnp.bfloat16), jnp.stack(dec_gain_grads))
```

```python
import functools
import math

import jax
import jax.numpy as jnp
from jax import lax
from jax.experimental import pallas as pl
from jax.experimental.pallas import tpu as pltpu
from jax.sharding import PartitionSpec as P

TSTEPS = 1000
EPS = 1e-06
GELU_SCALE = math.sqrt(2.0 / math.pi)
CUBIC = 0.044715
LANES = 128
MB_SAMPLES = 1
BF = jnp.bfloat16
F32 = jnp.float32


def dot(a, b):
    return jnp.dot(a, b, preferred_element_type=F32)


def left_dot(a, b):
    return lax.dot_general(a, b, (((0,), (0,)), ((), ())), preferred_element_type=F32)


def right_dot(a, b):
    return lax.dot_general(a, b, (((1,), (1,)), ((), ())), preferred_element_type=F32)


def plan(step_ids):
    angles = 0.5 * math.pi * (step_ids.astype(F32) + 0.5) / TSTEPS
    return jnp.cos(angles), jnp.sin(angles)


def features(step_ids, channels):
    half_width = channels // 2
    frequency = jnp.exp(-math.log(10000.0) * jnp.arange(half_width, dtype=F32) / half_width)
    angles = step_ids.astype(F32)[:, None] * frequency[None, :]
    return jnp.concatenate([jnp.sin(angles), jnp.cos(angles)], axis=1)


def normalize(rows):
    v = rows.astype(F32)
    inverse = lax.rsqrt(jnp.mean(v * v, axis=-1, keepdims=True) + EPS)
    return v * inverse, inverse


def norm_back(r, unit, inverse):
    return (r - unit * jnp.mean(r * unit, axis=-1, keepdims=True)) * inverse


def gelu_and_slope(p):
    square = p * p
    tanh = jnp.tanh(GELU_SCALE * (p + CUBIC * square * p))
    half = 0.5 * (1.0 + tanh)
    slope = half + 0.5 * p * (1.0 - tanh * tanh) * (GELU_SCALE * (1.0 + 3.0 * CUBIC * square))
    return p * half, slope


def mixed(rates, first, clean, noise):
    start, target = [], []
    for k in range(clean.shape[0]):
        keep, spread = rates[0, first + k], rates[1, first + k]
        c, n = clean[k].astype(F32), noise[k].astype(F32)
        start.append((keep * c + spread * n).astype(BF))
        target.append(keep * n - spread * c)
    if len(start) == 1:
        return start[0], target[0]
    return jnp.concatenate(start, 0), jnp.concatenate(target, 0)


def block_of(hidden):
    for width in (256, 128):
        if hidden % width == 0:
            return width
    return hidden


def embed_rows(emb, first, samples, row_count):
    rows = [jnp.broadcast_to(emb[first + k : first + k + 1, :], (row_count, emb.shape[1])) for k in range(samples)]
    return rows[0] if samples == 1 else jnp.concatenate(rows, 0)


def encode(x, emb, gain, w_in, w_out, a_ref, h_ref, slope_ref, unit_ref):
    unit, _ = normalize(x)
    unit_ref[...] = unit
    a = (unit * gain + emb).astype(BF)
    a_ref[...] = a
    width = block_of(w_in.shape[1])
    total = x.astype(F32)
    for j in range(0, w_in.shape[1], width):
        act, slope = gelu_and_slope(dot(a, w_in[:, j : j + width]))
        h = act.astype(BF)
        h_ref[:, j : j + width] = h
        slope_ref[:, j : j + width] = slope
        total = total + dot(h, w_out[j : j + width, :])
    return total.astype(BF)


def encode_back(g, gain, w_in, w_out, slope_ref, unit, gp_ref, gain_ref):
    width = block_of(w_in.shape[1])
    q = None
    for j in range(0, w_in.shape[1], width):
        gh = right_dot(g, w_out[j : j + width, :])
        gp = (gh * slope_ref[:, j : j + width]).astype(BF)
        gp_ref[:, j : j + width] = gp
        part = right_dot(gp, w_in[:, j : j + width])
        q = part if q is None else q + part
    gain_ref[...] = jnp.sum(q * unit, axis=0, keepdims=True)
    return q * gain


def decode(x, skip, gain_x, gain_s, weight):
    c = x.shape[1]
    ux = (normalize(x)[0] * gain_x).astype(BF)
    us = (normalize(skip)[0] * gain_s).astype(BF)
    y = x.astype(F32) + dot(ux, weight[:c, :]) + dot(us, weight[c:, :])
    return y.astype(BF), ux, us


class Call:
    def __init__(self):
        self.arrays, self.specs, self.names = [], [], []

    def add(self, name, array, block=None, index=None, space=None):
        if space is not None:
            spec = pl.BlockSpec(memory_space=space)
        elif block is None:
            spec = pl.BlockSpec(array.shape, functools.partial(lambda n, i: (0,) * n, array.ndim))
        else:
            spec = pl.BlockSpec(block, functools.partial(lambda at, i: at, index))
        self.arrays.append(array)
        self.specs.append(spec)
        self.names.append(name)

    def run(self, kernel, outs, scratch=(), name=None):
        out_names = list(outs)
        shapes = [jax.ShapeDtypeStruct(*outs[n]) for n in out_names]
        out_specs = [
            pl.BlockSpec(s.shape, functools.partial(lambda n, i: (0,) * n, len(s.shape))) for s in shapes
        ]
        n_in, n_out = len(self.names), len(out_names)

        def wrapped(*refs):
            table = dict(zip(self.names, refs[:n_in]))
            table.update(zip(out_names, refs[n_in : n_in + n_out]))
            kernel(table, *refs[n_in + n_out :])

        wrapped.__name__ = name
        done = pl.pallas_call(
            wrapped,
            grid=(1,),
            in_specs=self.specs,
            out_specs=out_specs,
            out_shape=shapes,
            scratch_shapes=list(scratch),
            name=name,
            compiler_params=pltpu.CompilerParams(vmem_limit_bytes=48 * 1024 * 1024),
        )(*self.arrays)
        return dict(zip(out_names, done))


def pack(ref, value, lane):
    m, c = value.shape
    full, rest = c // LANES, c % LANES
    for j in range(full):
        ref[j * m : (j + 1) * m, lane : lane + LANES] = value[:, j * LANES : (j + 1) * LANES]
    if rest:
        fold = LANES // rest
        part = m // fold
        for k in range(fold):
            ref[full * m : full * m + part, lane + k * rest : lane + (k + 1) * rest] = value[
                k * part : (k + 1) * part, full * LANES :
            ]


def unpack(rows, m, c):
    full, rest = c // LANES, c % LANES
    pieces = [rows[j * m : (j + 1) * m] for j in range(full)]
    if rest:
        fold = LANES // rest
        tail = rows[full * m :]
        pieces.append(jnp.concatenate([tail[:, k * rest : (k + 1) * rest] for k in range(fold)], axis=0))
    return jnp.concatenate(pieces, axis=1)


def split_halves(table, scratch, place):
    half = scratch.shape[0] // 2
    core = place[1]
    mine = pl.multiple_of(core * half, 8)
    other = pl.multiple_of((1 - core) * half, 8)
    table["kept"][...] = scratch[pl.ds(mine, half), :]
    table["sent"][...] = scratch[pl.ds(other, half), :].astype(table["sent"].dtype)


def bit_orders(devices):
    bits = list(range(1, devices.bit_length() - 1))
    return bits, bits[1:] + bits[:1]


def swap_bits(value, devices, first, second):
    pairs = [(i, i ^ (1 << (second if i & 1 else first))) for i in range(devices)]
    return lax.ppermute(value, "dp", pairs)


def side_of(device, first, second):
    odd = (device & 1) == 1
    return jnp.where(odd, (device >> second) & 1, (device >> first) & 1) == 1


def scatter_sum(kept, sent, devices, device):
    total = kept + lax.ppermute(sent, "dp", [(i, i ^ 1) for i in range(devices)]).astype(F32)
    for first, second in zip(*bit_orders(devices)):
        half = total.shape[0] // 2
        up = side_of(device, first, second)
        low, high = total[:half], total[half:]
        other = swap_bits(jnp.where(up, low, high).astype(BF), devices, first, second)
        total = jnp.where(up, high, low) + other.astype(F32)
    return total


def gather_shards(shard, devices, device):
    rows = shard[None]
    for first, second in reversed(list(zip(*bit_orders(devices)))):
        other = swap_bits(rows, devices, first, second)
        up = side_of(device, first, second)
        rows = jnp.concatenate([jnp.where(up, other, rows), jnp.where(up, rows, other)], 0)
    other = lax.ppermute(rows, "dp", [(i, i ^ 1) for i in range(devices)])
    up = (device & 1) == 1
    return jnp.concatenate([jnp.where(up, other, rows), jnp.where(up, rows, other)], 0)


def two_parts(vector):
    pad = -vector.shape[0] % LANES
    v = jnp.pad(vector, (0, pad)).reshape(-1, LANES)
    high = lax.reduce_precision(v, 8, 7)
    return jnp.concatenate([high, v - high], 0).astype(BF)


def one_vector(rows, length):
    k = rows.shape[1] // 2
    v = rows[:, :k].astype(F32) + rows[:, k:].astype(F32)
    return jnp.sum(v, axis=0).reshape(-1)[:length]


def body(clean, noise, timesteps, enc_in, enc_out, enc_gain, time_gain, dec_w, dec_gain):
    levels = lax.axis_size("pipe")
    devices = lax.axis_size("dp")
    level = lax.axis_index("pipe")
    device = lax.axis_index("dp")
    batches, row_count, channels = clean.shape
    hidden = enc_in.shape[2]
    total_rows = batches * devices * row_count
    samples = MB_SAMPLES if batches % MB_SAMPLES == 0 and levels <= 2 else batches
    groups = batches // samples
    rows = samples * row_count
    top = levels - 1

    keep_rate, spread = plan(timesteps)
    rates = jnp.stack([keep_rate, spread])
    embedding = time_gain * features(timesteps, channels)
    place = jnp.stack([level, device & 1]).astype(jnp.int32)

    w_half = dec_w.shape[1] // 2
    dec_ws, dec_gs = [], []
    for l in range(top):
        odd = (device & 1) == 1
        mine = jnp.where(odd, dec_w[0, w_half:], dec_w[0, :w_half])
        here = lax.ppermute(mine, "pipe", [(l, top)])
        other = lax.ppermute(here, "dp", [(i, i ^ 1) for i in range(devices)])
        dec_ws.append(
            jnp.concatenate([jnp.where(odd, other, here), jnp.where(odd, here, other)], 0)
        )
        dec_gs.append(lax.ppermute(dec_gain, "pipe", [(l, top)]))
    dec_ws.append(dec_w[0])
    dec_gs.append(dec_gain)

    def base(m, with_inputs):
        call = Call()
        call.add("place", place, space=pltpu.SMEM)
        call.add("rates", rates, space=pltpu.SMEM)
        if with_inputs:
            call.add("clean", clean, (samples, row_count, channels), (m, 0, 0))
            call.add("noise", noise, (samples, row_count, channels), (m, 0, 0))
        return call

    def weights(call):
        call.add("w_in", enc_in)
        call.add("w_out", enc_out)
        call.add("gain", enc_gain)

    fwd_outs = {
        "a": ((rows, channels), BF),
        "h": ((rows, hidden), BF),
        "slope": ((rows, hidden), F32),
        "unit": ((rows, channels), F32),
    }

    def input_rows(t, s, m):
        if s == 0:
            return mixed(t["rates"], m * samples, t["clean"][...], t["noise"][...])[0]
        return t["x"][...]

    def forward(s, m, x):
        call = base(m, s == 0)
        if s > 0:
            call.add("x", x)
        call.add("emb", embedding)
        weights(call)

        def kernel(t):
            @pl.when(t["place"][0] == s)
            def _():
                emb = embed_rows(t["emb"], m * samples, samples, row_count)
                t["y"][...] = encode(
                    input_rows(t, s, m), emb, t["gain"][...], t["w_in"].at[0], t["w_out"].at[0],
                    t["a"], t["h"], t["slope"], t["unit"],
                )

        return call.run(kernel, {"y": ((rows, channels), BF), **fwd_outs}, name=f"enc{s}")

    def top_forward(m, x):
        call = base(m, top == 0)
        if top > 0:
            call.add("x", x)
        call.add("emb", embedding)
        weights(call)
        call.add("dw", dec_ws[top])
        call.add("dg", dec_gs[top])

        def kernel(t):
            @pl.when(t["place"][0] == top)
            def _():
                emb = embed_rows(t["emb"], m * samples, samples, row_count)
                x = input_rows(t, top, m)
                y = encode(
                    x, emb, t["gain"][...], t["w_in"].at[0], t["w_out"].at[0],
                    t["a"], t["h"], t["slope"], t["unit"],
                )
                t["y"][...] = y
                z, ux, us = decode(y, x, t["dg"][:, :channels], t["dg"][:, channels:], t["dw"])
                t["z"][...] = z
                t[f"ux{top}"][...] = ux
                t[f"us{top}"][...] = us

        small = ((rows, channels), BF)
        outs = {"y": small, "z": small, f"ux{top}": small, f"us{top}": small, **fwd_outs}
        return call.run(kernel, outs, name="top_fwd")

    def top_rest(m, skips, ahead):
        call = base(m, True)
        for l in range(1, levels):
            call.add(f"x{l}", skips[l])
        for name in ("y", "z", "slope", "unit"):
            call.add(name, ahead[name])
        weights(call)
        for l in range(levels):
            call.add(f"dw{l}", dec_ws[l])
            call.add(f"dg{l}", dec_gs[l])

        def kernel(t):
            @pl.when(t["place"][0] == top)
            def _():
                start, target = mixed(t["rates"], m * samples, t["clean"][...], t["noise"][...])
                skip = [start] + [t[f"x{l}"][...] for l in range(1, levels)]
                z = [None] * (levels + 1)
                z[levels], z[top] = t["y"][...], t["z"][...]
                for l in range(top - 1, -1, -1):
                    dg = t[f"dg{l}"]
                    z[l], ux, us = decode(z[l + 1], skip[l], dg[:, :channels], dg[:, channels:], t[f"dw{l}"])
                    t[f"ux{l}"][...] = ux
                    t[f"us{l}"][...] = us
                residual = z[0].astype(F32) - target
                t["loss"][...] = jnp.sum(residual * residual, axis=0, keepdims=True)
                g = (residual / math.sqrt(total_rows)).astype(BF)
                back_s = None
                for l in range(levels):
                    t[f"gd{l}"][...] = g
                    dw, dg = t[f"dw{l}"], t[f"dg{l}"]
                    unit_x, inv_x = normalize(z[l + 1])
                    unit_s, inv_s = normalize(skip[l])
                    qx = right_dot(g, dw[:channels, :])
                    qs = right_dot(g, dw[channels:, :])
                    t["dgain"][2 * l : 2 * l + 1, :] = jnp.sum(qx * unit_x, axis=0, keepdims=True)
                    t["dgain"][2 * l + 1 : 2 * l + 2, :] = jnp.sum(qs * unit_s, axis=0, keepdims=True)
                    if l > 0:
                        back_s = norm_back(qs * dg[:, channels:], unit_s, inv_s)
                        if l < top:
                            t[f"back{l}"][...] = back_s
                    gx = g.astype(F32) + norm_back(qx * dg[:, :channels], unit_x, inv_x)
                    g = gx.astype(BF)
                t["g"][...] = g
                unit = t["unit"][...]
                r = encode_back(
                    g, t["gain"][...], t["w_in"].at[0], t["w_out"].at[0], t["slope"], unit, t["gp"], t["egain"]
                )
                if top > 0:
                    _, inverse = normalize(skip[top])
                    t["down"][...] = (g.astype(F32) + norm_back(r, unit, inverse) + back_s).astype(BF)

        small = ((rows, channels), BF)
        outs = {"g": small, "gp": ((rows, hidden), BF), "egain": ((1, channels), F32)}
        outs["loss"] = ((1, channels), F32)
        outs["dgain"] = ((2 * levels, channels), F32)
        if top > 0:
            outs["down"] = small
        for l in range(levels):
            outs[f"gd{l}"] = small
            if l < top:
                outs[f"ux{l}"] = small
                outs[f"us{l}"] = small
            if 0 < l < top:
                outs[f"back{l}"] = ((rows, channels), F32)
        return call.run(kernel, outs, name="top_rest")

    def backward(s, m, g, ahead, x, back_s):
        call = base(m, False)
        call.add("g", g)
        call.add("slope", ahead["slope"])
        call.add("unit", ahead["unit"])
        weights(call)
        if s > 0:
            call.add("x", x)
            call.add("back", back_s)

        def kernel(t):
            @pl.when(t["place"][0] == s)
            def _():
                g = t["g"][...]
                unit = t["unit"][...]
                r = encode_back(
                    g, t["gain"][...], t["w_in"].at[0], t["w_out"].at[0], t["slope"], unit, t["gp"], t["egain"]
                )
                if s > 0:
                    _, inverse = normalize(t["x"][...])
                    t["down"][...] = (g.astype(F32) + norm_back(r, unit, inverse) + t["back"][...]).astype(BF)

        outs = {"gp": ((rows, hidden), BF), "egain": ((1, channels), F32)}
        if s > 0:
            outs["down"] = ((rows, channels), BF)
        return call.run(kernel, outs, name=f"enc_back{s}")

    def enc_grad(lefts, rights, m_out, n_out, name):
        packed = m_out * n_out // LANES
        call = Call()
        call.add("place", place, space=pltpu.SMEM)
        sources = len(lefts)
        for s in range(sources):
            for m in range(groups):
                call.add(f"l{s}_{m}", lefts[s][m], space=pl.ANY)
                call.add(f"r{s}_{m}", rights[s][m], space=pl.ANY)

        def kernel(t, left, right, scratch, sems):
            for s in range(sources):
                @pl.when((t["place"][0] == s) | (sources == 1))
                def _():
                    copies = []
                    for m in range(groups):
                        at = pl.ds(m * rows, rows)
                        copies.append(pltpu.make_async_copy(t[f"l{s}_{m}"], left.at[at], sems.at[2 * m]))
                        copies.append(pltpu.make_async_copy(t[f"r{s}_{m}"], right.at[at], sems.at[2 * m + 1]))
                    for copy in copies:
                        copy.start()
                    for copy in copies:
                        copy.wait()
            pack(scratch, left_dot(left[...], right[...]), 0)
            split_halves(t, scratch, t["place"])

        return call.run(
            kernel,
            {"kept": ((packed // 2, LANES), F32), "sent": ((packed // 2, LANES), F32)},
            scratch=[
                pltpu.VMEM((groups * rows, m_out), BF),
                pltpu.VMEM((groups * rows, n_out), BF),
                pltpu.VMEM((packed, LANES), F32),
                pltpu.SemaphoreType.DMA((2 * groups,)),
            ],
            name=name,
        )

    def dec_grad(ux, us, gd):
        packed = 2 * channels * channels // LANES
        call = Call()
        call.add("place", place, space=pltpu.SMEM)
        for l in range(levels):
            for m in range(groups):
                call.add(f"ux{l}_{m}", ux[l][m])
                call.add(f"us{l}_{m}", us[l][m])
                call.add(f"g{l}_{m}", gd[l][m])

        def kernel(t, scratch):
            @pl.when(t["place"][0] == top)
            def _():
                for l in range(levels):
                    def joined(kind):
                        parts = [t[f"{kind}{l}_{m}"][...] for m in range(groups)]
                        return parts[0] if groups == 1 else jnp.concatenate(parts, 0)
                    g = joined("g")
                    both = jnp.concatenate([left_dot(joined("ux"), g), left_dot(joined("us"), g)], 0)
                    pack(scratch, both, l * LANES)
                split_halves(t, scratch, t["place"])

        shape = (packed // 2, levels * LANES)
        return call.run(
            kernel,
            {"kept": (shape, F32), "sent": (shape, F32)},
            scratch=[pltpu.VMEM((packed, levels * LANES), F32)],
            name="dec_grad",
        )

    merged = levels > 2
    entries = 1 if merged else levels
    ahead, gs, gps, gains = ([[None] * groups for _ in range(entries)] for _ in range(4))

    def put(slots, s, m, value):
        if not merged:
            slots[s][m] = value
        elif slots[0][m] is None:
            slots[0][m] = value
        else:
            slots[0][m] = lax.optimization_barrier(
                jax.tree.map(lambda new, old: jnp.where(level == s, new, old), value, slots[0][m])
            )

    def get(slots, s, m):
        return slots[0 if merged else s][m]

    def kept_of(done):
        return {name: done[name] for name in fwd_outs}

    xs = [[None] * (levels + 1) for _ in range(groups)]
    for wave in range(top + groups - 1 if top else 0):
        for s in range(top):
            m = wave - s
            if not 0 <= m < groups:
                continue
            done = forward(s, m, xs[m][s])
            put(ahead, s, m, kept_of(done))
            xs[m][s + 1] = done["y"]
            for l in range(1, s + 2):
                xs[m][l] = lax.ppermute(xs[m][l], "pipe", [(s, s + 1)])
    rest, last = [None] * groups, [None] * groups
    for m in range(groups):
        last[m] = top_forward(m, xs[m][top])
        put(ahead, top, m, kept_of(last[m]))
    for m in range(groups):
        rest[m] = top_rest(m, xs[m], last[m])
        put(gs, top, m, rest[m]["g"])
        put(gps, top, m, rest[m]["gp"])
        put(gains, top, m, rest[m]["egain"])
    for m in range(groups):
        g = rest[m].get("down")
        for s in range(top - 1, -1, -1):
            g = lax.ppermute(g, "pipe", [(s + 1, s)])
            put(gs, s, m, g)
            back_s = None
            if s > 0:
                back_s = rest[m][f"back{s}"]
                for hop in range(top, s, -1):
                    back_s = lax.ppermute(back_s, "pipe", [(hop, hop - 1)])
            done = backward(s, m, g, get(ahead, s, m), xs[m][s], back_s)
            put(gps, s, m, done["gp"])
            put(gains, s, m, done["egain"])
            g = done.get("down")
    lefts_out = [[ahead[s][m]["h"] for m in range(groups)] for s in range(entries)]

    ux = [[(last if l == top else rest)[m][f"ux{l}"] for m in range(groups)] for l in range(levels)]
    us = [[(last if l == top else rest)[m][f"us{l}"] for m in range(groups)] for l in range(levels)]
    gd = [[rest[m][f"gd{l}"] for m in range(groups)] for l in range(levels)]
    dec = dec_grad(ux, us, gd)
    dec_sum = scatter_sum(dec["kept"], dec["sent"], devices, device)
    dgain = sum(rest[m]["dgain"] for m in range(groups))
    loss = jnp.sum(sum(rest[m]["loss"] for m in range(groups)))
    loss_row = jnp.pad(loss[None], (0, LANES - 1))
    dec_shard = None
    for l in range(levels):
        extra = two_parts(jnp.concatenate([jnp.pad(dgain[2 * l : 2 * l + 2].reshape(-1), (0, -2 * channels % LANES)), loss_row]))
        shard = jnp.concatenate([dec_sum[:, l * LANES : (l + 1) * LANES].astype(BF), extra], 0)
        if l < top:
            shard = lax.ppermute(shard, "pipe", [(top, l)])
        dec_shard = shard if dec_shard is None else jnp.where(level == l, shard, dec_shard)

    egain = None
    for s in range(entries):
        mine = sum(gains[s][m] for m in range(groups))
        egain = mine if egain is None else jnp.where(level == s, mine, egain)
    gain_rows = two_parts(egain[0])

    out_parts = enc_grad(lefts_out, gs, hidden, channels, "grad_out")
    out_sum = scatter_sum(out_parts["kept"], out_parts["sent"], devices, device)
    lefts_in = [[ahead[s][m]["a"] for m in range(groups)] for s in range(entries)]
    in_parts = enc_grad(lefts_in, gps, channels, hidden, "grad_in")
    in_sum = scatter_sum(in_parts["kept"], in_parts["sent"], devices, device)

    n_out, n_dec, n_in = out_sum.shape[0], dec_sum.shape[0], in_sum.shape[0]
    first = gather_shards(jnp.concatenate([out_sum.astype(BF), dec_shard], 0), devices, device)
    second = gather_shards(jnp.concatenate([in_sum.astype(BF), gain_rows], 0), devices, device)

    g_out = unpack(first[:, :n_out].reshape(-1, LANES), hidden, channels)
    g_dec = unpack(first[:, n_out : n_out + n_dec].reshape(-1, LANES), 2 * channels, channels)
    g_in = unpack(second[:, :n_in].reshape(-1, LANES), channels, hidden)
    dec_vec = one_vector(first[:, n_out + n_dec :], 2 * channels + (-2 * channels % LANES) + LANES)
    g_egain = one_vector(second[:, n_in:], channels)
    loss_at = dec_vec.shape[0] - LANES
    return (
        dec_vec[loss_at] / (total_rows * channels),
        g_in[None],
        g_out[None],
        g_egain[None],
        g_dec[None],
        dec_vec[: 2 * channels][None],
    )


def solution(mesh):
    in_specs = (
        P("dp", None, None),
        P("dp", None, None),
        P("dp"),
        P("pipe", None, None),
        P("pipe", None, None),
        P("pipe", None),
        P("pipe", None),
        P("pipe", None, None),
        P("pipe", None),
    )
    out_specs = (
        P(),
        P("pipe", None, None),
        P("pipe", None, None),
        P("pipe", None),
        P("pipe", None, None),
        P("pipe", None),
    )
    return jax.shard_map(body, mesh=mesh, in_specs=in_specs, out_specs=out_specs, check_vma=False)
```
